32 devices in a mesh: fsdp: 2 (over x), ctx: 4 (over y, core), tp: 4 (over z).
Axes of the slice: x: 2, y: 2, z: 4, core: 2. Of those that a mesh axis runs over, the one named last changes fastest.
Arguments:
- inputs: bfloat16 [8, 2048, 768], P('fsdp', ('ctx', 'tp')), may hold values from -6 to 6
- segments: int32 [8, 2048], P('fsdp'), may hold values from 0 to 15, never falling along the last dimension, each value on 1 to 1024 neighbouring positions
- query_weight: bfloat16 [768, 768], P(('fsdp', 'ctx'), 'tp'), may hold values from -0.3125 to 0.3125
- query_bias: float32 [768], P('tp'), may hold values from -1.5 to 1.5
- key_weight: bfloat16 [768, 768], P(('fsdp', 'ctx'), 'tp'), may hold values from -0.3125 to 0.3125
- value_weight: bfloat16 [768, 768], P(('fsdp', 'ctx'), 'tp'), may hold values from -0.21875 to 0.21875
- value_bias: float32 [768], P('tp'), may hold values from -1.5 to 1.5
- output_weight: bfloat16 [768, 768], P('tp', ('fsdp', 'ctx')), may hold values from -1.25 to 1.25
- output_bias: float32 [768], replicated, may hold values from -1.5 to 1.5
- first_gain: float32 [768], replicated, may hold values from 0.5 to 1.5
- first_shift: float32 [768], replicated, may hold values from -1.5 to 1.5
- expand_weight: bfloat16 [768, 3072], P(('fsdp', 'ctx'), 'tp'), may hold values from -0.21875 to 0.21875
- expand_bias: float32 [3072], P('tp'), may hold values from -1.5 to 1.5
- contract_weight: bfloat16 [3072, 768], P('tp', ('fsdp', 'ctx')), may hold values from -0.15625 to 0.15625
- contract_bias: float32 [768], replicated, may hold values from -1.5 to 1.5
- second_gain: float32 [768], replicated, may hold values from 0.5 to 1.5
- second_shift: float32 [768], replicated, may hold values from -1.5 to 1.5
- cotangent: bfloat16 [8, 2048, 768], P('fsdp', ('ctx', 'tp')), may hold values from -6 to 6
Outputs:
- outputs: bfloat16 [8, 2048, 768], P('fsdp', ('ctx', 'tp'))
- input_grad: bfloat16 [8, 2048, 768], P('fsdp', ('ctx', 'tp'))
- query_weight_grad: float32 [768, 768], P(('fsdp', 'ctx'), 'tp')
- query_bias_grad: float32 [768], P('tp')
- key_weight_grad: float32 [768, 768], P(('fsdp', 'ctx'), 'tp')
- value_weight_grad: float32 [768, 768], P(('fsdp', 'ctx'), 'tp')
- value_bias_grad: float32 [768], P('tp')
- output_weight_grad: float32 [768, 768], P('tp', ('fsdp', 'ctx'))
- output_bias_grad: float32 [768], replicated
- first_gain_grad: float32 [768], replicated
- first_shift_grad: float32 [768], replicated
- expand_weight_grad: float32 [768, 3072], P(('fsdp', 'ctx'), 'tp')
- expand_bias_grad: float32 [3072], P('tp')
- contract_weight_grad: float32 [3072, 768], P('tp', ('fsdp', 'ctx'))
- contract_bias_grad: float32 [768], replicated
- second_gain_grad: float32 [768], replicated
- second_shift_grad: float32 [768], replicated
The draws below stay inside these ranges and needn't reach their ends.
Inputs may be any that keep to these rules, and one draw needn't show every extreme that they name: `segments`: along each sequence the segment numbers never fall and take every value 0 to 15; a document has at most 1024 tokens, and one document of each sequence has exactly 1024.
All inputs are finite; a program needn't handle non-finite values.
Results may differ from the reference program's by a relative error of at most 0.022.
Values may be sent and summed in bfloat16 or wider, within the bound.
No kernel may reach another device: no remote copies, remote signals or barrier semaphores. Data moves between devices by JAX's collectives and lax.ppermute only.
A program may use at most 192 MiB of HBM per device.

```python
import math
import jax
import jax.numpy as jnp
import numpy as np
from jax import lax

D = 768
HEADS = 12
HEAD_DIM = 64
FF = 3072
SEQ_LEN = 2048
DOCS = 16
DOC_MOST = 1024
SEQS = 8


def block_scale(rng, extent, split, least, top_value):
    level, own = 1.0, jax.random.fold_in(rng, 6)
    for dim, shards_of in split:
        heights = jnp.exp(jax.random.uniform(jax.random.fold_in(own, dim), (shards_of,), jnp.float32, least / len(split), top_value / len(split)))
        level = level * jnp.repeat(heights, extent[dim] // shards_of).reshape([-1 if axis == dim else 1 for axis in range(len(extent))])
    return level


def length_profile(number_of, total, reach, lean):
    weights = [(1 << 20) // math.isqrt(grade ** lean) + 1 for grade in range(2, number_of + 1)]
    spare, given = total - reach - (number_of - 1), [1] * (number_of - 1)
    while spare > 0:
        free = [i for i in range(number_of - 1) if given[i] < reach]
        mass, left = sum([weights[i] for i in free]), spare
        for i in free:
            addition = min(reach - given[i], max(1, left * weights[i] // mass), spare)
            given[i] = given[i] + addition
            spare = spare - addition
    return np.array([reach] + given)


def uneven(own_key, count, total, limit, slope):
    if count == 2:
        one = jax.random.randint(own_key, (), max(1, total - limit), min(limit, total - 1) + 1)
        return jnp.stack([one, total - one])
    lengths = jnp.asarray(length_profile(count, total, limit, slope), jnp.int32)
    couples = (count - 1) // 2
    donor, receiver = lengths[1:1 + 2 * couples:2], lengths[2:2 + 2 * couples:2]
    room = jnp.minimum(donor - 1, limit - receiver)
    moved = jax.random.randint(jax.random.fold_in(own_key, 1), (couples,), 0, 1 << 20) % (room + 1)
    lengths = lengths.at[1:1 + 2 * couples:2].set(donor - moved).at[2:2 + 2 * couples:2].set(receiver + moved)
    return lengths[jax.random.permutation(jax.random.fold_in(own_key, 2), count)]


def normal_values(rng, extent, scale, bound, shards=(), dtype=jnp.bfloat16):
    values = scale * jax.random.normal(rng, extent, jnp.float32)
    if shards:
        values = values * block_scale(rng, extent, shards, -0.22, 0.18)
    return jnp.clip(values, -bound, bound).astype(dtype)


def setup_inputs(seed: int = 0) -> dict:
    streams_of = jax.random.split(jax.random.key(seed), 19)
    return {
        "inputs": normal_values(streams_of[0], (SEQS, SEQ_LEN, D), 1.0, 6.0, ((0, 2), (1, 16))),
        "segments": jax.vmap(lambda own: jnp.searchsorted(jnp.cumsum(uneven(own, DOCS, SEQ_LEN, DOC_MOST, 2)), jnp.arange(SEQ_LEN), side="right"))(jax.random.split(streams_of[1], SEQS)).reshape((SEQS, SEQ_LEN)).astype(jnp.int32),
        "query_weight": normal_values(streams_of[2], (D, D), (D // 2) ** -0.5, 0.3125, ((0, 8), (1, 4))),
        "query_bias": normal_values(streams_of[3], (D,), 0.3, 1.5, ((0, 4),), jnp.float32),
        "key_weight": normal_values(streams_of[4], (D, D), (D // 2) ** -0.5, 0.3125, ((0, 8), (1, 4))),
        "value_weight": normal_values(streams_of[5], (D, D), D ** -0.5, 0.21875, ((0, 8), (1, 4))),
        "value_bias": normal_values(streams_of[6], (D,), 0.3, 1.5, ((0, 4),), jnp.float32),
        "output_weight": normal_values(streams_of[7], (D, D), (D // 32) ** -0.5, 1.25, ((0, 4), (1, 8))),
        "output_bias": normal_values(streams_of[8], (D,), 0.3, 1.5, (), jnp.float32),
        "first_gain": jnp.clip(1.0 + 0.1 * jax.random.normal(streams_of[9], (D,), jnp.float32), 0.5, 1.5),
        "first_shift": normal_values(streams_of[10], (D,), 0.3, 1.5, (), jnp.float32),
        "expand_weight": normal_values(streams_of[11], (D, FF), D ** -0.5, 0.21875, ((0, 8), (1, 4))),
        "expand_bias": normal_values(streams_of[12], (FF,), 0.3, 1.5, ((0, 4),), jnp.float32),
        "contract_weight": normal_values(streams_of[13], (FF, D), (FF // 2) ** -0.5, 0.15625, ((0, 4), (1, 8))),
        "contract_bias": normal_values(streams_of[14], (D,), 0.3, 1.5, (), jnp.float32),
        "second_gain": jnp.clip(1.0 + 0.1 * jax.random.normal(streams_of[15], (D,), jnp.float32), 0.5, 1.5),
        "second_shift": normal_values(streams_of[16], (D,), 0.3, 1.5, (), jnp.float32),
        "cotangent": normal_values(streams_of[17], (SEQS, SEQ_LEN, D), 1.0, 6.0, ((0, 2), (1, 16))),
    }


@jax.custom_vjp
def low(v):
    return lax.optimization_barrier(v.astype(jnp.bfloat16)).astype(jnp.float32)

@jax.custom_vjp
def low_back(v):
    return v

def low_keep(v):
    return (low(v), None)

def low_pass(kept, grad):
    return (grad,)

def back_keep(v):
    return (v, None)

def back_low(kept, grad):
    return (low(grad),)
low.defvjp(low_keep, low_pass)
low_back.defvjp(back_keep, back_low)
epsilon = 1e-05
masked_value = -1e+30

def both_ways(value):
    return low(low_back(value))

def product(left, right):
    return jnp.dot(left, right, precision=lax.Precision.HIGHEST, preferred_element_type=jnp.float32)

def layer_norm(resid, gain, shift):
    row_mean = lax.optimization_barrier(jnp.mean(resid, axis=-1, keepdims=True))
    spread = lax.optimization_barrier(jnp.mean(resid * resid, axis=-1, keepdims=True)) - row_mean * row_mean
    return (resid - row_mean) * lax.rsqrt(spread + epsilon) * gain + shift

def split_heads(tensor):
    return tensor.reshape(SEQ_LEN, HEADS, HEAD_DIM).transpose(1, 0, 2)

def encoder_layer(params, tokens, segment_row):
    query_weight, query_bias, key_weight, value_weight, value_bias, output_weight, output_bias, first_gain, first_shift, expand_weight, expand_bias, contract_weight, contract_bias, second_gain, second_shift = params
    queries = both_ways(product(tokens, query_weight) + query_bias)
    key_rows = both_ways(product(tokens, key_weight))
    value_rows = both_ways(product(tokens, value_weight) + value_bias)
    same_doc = segment_row[:, None] == segment_row[None, :]

    def one_head(pieces):
        head_query, head_keys, head_values = pieces
        scores = low_back(jnp.dot(head_query, head_keys.T, precision=lax.Precision.HIGHEST) * HEAD_DIM ** (-0.5))
        scores = jnp.where(same_doc, scores, masked_value)
        softmax_rows = low(jax.nn.softmax(scores, axis=-1))
        return jnp.dot(softmax_rows, head_values, precision=lax.Precision.HIGHEST)
    attended = lax.map(jax.checkpoint(one_head), (split_heads(queries), split_heads(key_rows), split_heads(value_rows)))
    attended = both_ways(attended.transpose(1, 0, 2).reshape(SEQ_LEN, D))
    branch = low_back(product(attended, output_weight) + output_bias)
    middle = layer_norm(tokens + branch, first_gain, first_shift)
    preact = low_back(product(low(middle), expand_weight) + expand_bias)
    active = low(jax.nn.gelu(preact, approximate=False))
    feedforward = low_back(product(active, contract_weight) + contract_bias)
    return layer_norm(middle + feedforward, second_gain, second_shift)

def reference(inputs, segments, query_weight, query_bias, key_weight, value_weight, value_bias, output_weight, output_bias, first_gain, first_shift, expand_weight, expand_bias, contract_weight, contract_bias, second_gain, second_shift, cotangent):
    params = tuple((weight.astype(jnp.float32) for weight in (query_weight, query_bias, key_weight, value_weight, value_bias, output_weight, output_bias, first_gain, first_shift, expand_weight, expand_bias, contract_weight, contract_bias, second_gain, second_shift)))

    def sequence_step(totals, entries):
        tokens, segment_row, upstream = entries
        result, pullback = jax.vjp(lambda values, tokens_float: encoder_layer(values, tokens_float, segment_row), params, tokens.astype(jnp.float32))
        param_grads, token_grad = pullback(upstream.astype(jnp.float32))
        totals = jax.tree.map(jnp.add, totals, param_grads)
        return (totals, (result.astype(jnp.bfloat16), token_grad.astype(jnp.bfloat16)))
    starts = tuple((jnp.zeros_like(weight) for weight in params))
    totals, (outputs, input_grad) = lax.scan(sequence_step, starts, (inputs, segments, cotangent))
    return (outputs, input_grad, totals[0], totals[1], totals[2], totals[3], totals[4], totals[5], totals[6], totals[7], totals[8], totals[9], totals[10], totals[11], totals[12], totals[13], totals[14])
```

```python
import functools

import jax
import jax.numpy as jnp
from jax import lax
from jax.experimental import pallas as pl
from jax.experimental.pallas import tpu as pltpu
from jax.sharding import PartitionSpec as P

HEAD_DIM = 64
TILE_Q = 256
TILE_K = 256

epsilon = 1e-05
masked_value = -1e30
bf16 = jnp.bfloat16
f32 = jnp.float32


def dot32(a, b, dims):
    return lax.dot_general(a, b, (dims, ((), ())), preferred_element_type=f32)


def swap(value, axis, bit):
    count = lax.axis_size(axis)
    return lax.ppermute(value, axis, [(i, i ^ bit) for i in range(count)])


def side(axis, bit):
    return (lax.axis_index(axis) & bit) != 0


def exchange_blocks(blocks, axis):
    count = lax.axis_size(axis)
    me = lax.axis_index(axis)
    got = []
    for k in range(1, count):
        send = lax.dynamic_index_in_dim(blocks, (me + k) % count, 0, keepdims=True)
        got.append(lax.ppermute(send, axis, [(i, (i + k) % count) for i in range(count)]))
    out = blocks
    for k in range(1, count):
        out = lax.dynamic_update_slice_in_dim(out, got[k - 1], (me - k) % count, 0)
    return out


def gather_line(value, axis):
    count = lax.axis_size(axis)
    me = lax.axis_index(axis)
    got = [
        lax.ppermute(value, axis, [(i, (i + k) % count) for i in range(count)])
        for k in range(1, count)
    ]
    out = jnp.broadcast_to(value[None], (count, *value.shape))
    for k in range(1, count):
        out = lax.dynamic_update_slice_in_dim(out, got[k - 1][None], (me - k) % count, 0)
    return out


def bits_of(axis):
    count = lax.axis_size(axis)
    bits, bit = [], 1
    while bit < count:
        bits.append(bit)
        bit *= 2
    return bits


def exchange_orders():
    ctx_bits = [("ctx", b) for b in bits_of("ctx")]
    fsdp_bits = [("fsdp", b) for b in bits_of("fsdp")]
    near, far = ctx_bits[:1], ctx_bits[1:]
    return (far + fsdp_bits + near, fsdp_bits + far + near)


def gather_rows(local):
    lines = gather_line(local, "tp")
    half = lines.shape[0] // 2
    done = []
    for color, order in enumerate(exchange_orders()):
        part = lines[color * half : (color + 1) * half]
        names = []
        for axis, bit in order:
            other = swap(part, axis, bit)
            mine_last = side(axis, bit)
            names.append((axis, bit))
            names.sort(key=lambda n: (n[0] == "ctx", -n[1]))
            at = 1 + names.index((axis, bit))
            part = jnp.where(
                mine_last, jnp.stack([other, part], at), jnp.stack([part, other], at)
            )
        done.append(part.reshape(half, -1, local.shape[1]))
    return jnp.concatenate(done, 0)


def scatter_rows(whole, rows):
    half = whole.shape[0] // 2
    left = []
    for color, order in enumerate(exchange_orders()):
        names = sorted(order, key=lambda n: (n[0] == "ctx", -n[1]))
        part = whole[color * half : (color + 1) * half]
        part = part.reshape(half, *([2] * len(names)), rows, whole.shape[2])
        for axis, bit in reversed(order):
            at = 1 + names.index((axis, bit))
            names.remove((axis, bit))
            low = lax.index_in_dim(part, 0, at, keepdims=False)
            high = lax.index_in_dim(part, 1, at, keepdims=False)
            upper = side(axis, bit)
            keep, send = jnp.where(upper, high, low), jnp.where(upper, low, high)
            other = swap(send, axis, bit)
            part = (keep.astype(f32) + other.astype(f32)).astype(bf16)
        left.append(part)
    lines = exchange_blocks(jnp.concatenate(left, 0), "tp")
    return jnp.sum(lines.astype(f32), axis=0)


def sum_everywhere(value):
    for axis in ("ctx", "fsdp", "tp"):
        for bit in bits_of(axis):
            value = value + swap(value, axis, bit)
    return value


def head_rows(value, head):
    row = lax.broadcasted_iota(jnp.int32, value.shape, 0)
    return jnp.where((row >= head * HEAD_DIM) & (row < (head + 1) * HEAD_DIM), value, 0)


def head_cols(value, head):
    col = lax.broadcasted_iota(jnp.int32, value.shape, 1)
    return jnp.where((col >= head * HEAD_DIM) & (col < (head + 1) * HEAD_DIM), value, 0)


def attend_kernel(
    low_ref, high_ref, q_ref, k_ref, v_ref, segr_ref, segc_ref, att_ref, attt_ref, lse_ref,
    vt_ref, acc_ref,
):
    tokens, width = q_ref.shape
    heads = width // HEAD_DIM
    scale = HEAD_DIM ** (-0.5)

    def turn(i, carry):
        at = pl.multiple_of(i * TILE_K, TILE_K)
        vt_ref[:, pl.ds(at, TILE_K)] = v_ref[pl.ds(at, TILE_K), :].astype(f32).T.astype(bf16)
        return carry

    lax.fori_loop(0, tokens // TILE_K, turn, 0)

    def one_q(i, carry):
        qa = pl.multiple_of(i * TILE_Q, TILE_Q)
        qt = (q_ref[pl.ds(qa, TILE_Q), :].astype(f32) * scale).T
        qts = [head_rows(qt, h).astype(bf16) for h in range(heads)]
        seg_q = segr_ref[:, pl.ds(qa, TILE_Q)]
        acc_ref[...] = jnp.zeros_like(acc_ref)

        def one_k(j, state):
            ka = pl.multiple_of(j * TILE_K, TILE_K)
            keys = k_ref[pl.ds(ka, TILE_K), :]
            same = segc_ref[pl.ds(ka, TILE_K), :] == seg_q
            tops, sums = [], []
            for h in range(heads):
                rows = slice(h * HEAD_DIM, (h + 1) * HEAD_DIM)
                s = jnp.where(same, dot32(keys, qts[h], ((1,), (0,))), masked_value)
                top = jnp.maximum(state[0][h], jnp.max(s, axis=0, keepdims=True))
                shrink = jnp.exp(state[0][h] - top)
                p = jnp.exp(s - top)
                sums.append(state[1][h] * shrink + jnp.sum(p, axis=0, keepdims=True))
                tops.append(top)
                pv = dot32(vt_ref[rows, pl.ds(ka, TILE_K)], p.astype(bf16), ((1,), (0,)))
                acc_ref[rows, :] = acc_ref[rows, :] * shrink + pv
            return (tuple(tops), tuple(sums))

        init = (
            tuple(jnp.full((1, TILE_Q), masked_value, f32) for _ in range(heads)),
            tuple(jnp.zeros((1, TILE_Q), f32) for _ in range(heads)),
        )
        tops, sums = lax.fori_loop(low_ref[i], high_ref[i], one_k, init)
        for h in range(heads):
            rows = slice(h * HEAD_DIM, (h + 1) * HEAD_DIM)
            acc_ref[rows, :] = acc_ref[rows, :] / sums[h]
            lse_ref[h : h + 1, pl.ds(qa, TILE_Q)] = tops[h] + jnp.log(sums[h])
        attt_ref[:, pl.ds(qa, TILE_Q)] = acc_ref[...]
        att_ref[pl.ds(qa, TILE_Q), :] = acc_ref[...].T.astype(bf16)
        return carry

    lax.fori_loop(0, tokens // TILE_Q, one_q, 0)


def attend_back_kernel(
    low_ref, high_ref, q_ref, k_ref, v_ref, do_ref, attt_ref, lse_ref, segr_ref, segc_ref,
    dq_ref, dk_ref, dv_ref, kt_ref, dqt_ref, dka_ref, dva_ref,
):
    tokens, width = q_ref.shape
    heads = width // HEAD_DIM
    scale = HEAD_DIM ** (-0.5)

    def turn(i, carry):
        at = pl.multiple_of(i * TILE_K, TILE_K)
        kt_ref[:, pl.ds(at, TILE_K)] = k_ref[pl.ds(at, TILE_K), :].astype(f32).T.astype(bf16)
        return carry

    lax.fori_loop(0, tokens // TILE_K, turn, 0)
    dka_ref[...] = jnp.zeros_like(dka_ref)
    dva_ref[...] = jnp.zeros_like(dva_ref)

    def one_q(i, carry):
        qa = pl.multiple_of(i * TILE_Q, TILE_Q)
        q = q_ref[pl.ds(qa, TILE_Q), :].astype(f32) * scale
        do = do_ref[pl.ds(qa, TILE_Q), :].astype(f32)
        qt, dot_ = q.T, do.T
        qs = [head_cols(q, h).astype(bf16) for h in range(heads)]
        dos = [head_cols(do, h).astype(bf16) for h in range(heads)]
        qts = [head_rows(qt, h).astype(bf16) for h in range(heads)]
        dots = [head_rows(dot_, h).astype(bf16) for h in range(heads)]
        prod = dot_ * attt_ref[:, pl.ds(qa, TILE_Q)]
        deltas = [
            jnp.sum(prod[h * HEAD_DIM : (h + 1) * HEAD_DIM, :], axis=0, keepdims=True)
            for h in range(heads)
        ]
        lses = [lse_ref[h : h + 1, pl.ds(qa, TILE_Q)] for h in range(heads)]
        seg_q = segr_ref[:, pl.ds(qa, TILE_Q)]
        dqt_ref[...] = jnp.zeros_like(dqt_ref)

        def one_k(j, state):
            ka = pl.multiple_of(j * TILE_K, TILE_K)
            keys = k_ref[pl.ds(ka, TILE_K), :]
            values = v_ref[pl.ds(ka, TILE_K), :]
            same = segc_ref[pl.ds(ka, TILE_K), :] == seg_q
            dk = dka_ref[pl.ds(ka, TILE_K), :]
            dv = dva_ref[pl.ds(ka, TILE_K), :]
            for h in range(heads):
                rows = slice(h * HEAD_DIM, (h + 1) * HEAD_DIM)
                s = jnp.where(same, dot32(keys, qts[h], ((1,), (0,))), masked_value)
                p = jnp.exp(s - lses[h])
                dp = dot32(values, dots[h], ((1,), (0,)))
                ds = (p * (dp - deltas[h])).astype(bf16)
                dv = dv + dot32(p.astype(bf16), dos[h], ((1,), (0,)))
                dk = dk + dot32(ds, qs[h], ((1,), (0,)))
                dqt_ref[rows, :] += dot32(kt_ref[rows, pl.ds(ka, TILE_K)], ds, ((1,), (0,)))
            dka_ref[pl.ds(ka, TILE_K), :] = dk
            dva_ref[pl.ds(ka, TILE_K), :] = dv
            return state

        lax.fori_loop(low_ref[i], high_ref[i], one_k, 0)
        dq_ref[pl.ds(qa, TILE_Q), :] = (dqt_ref[...] * scale).T.astype(bf16)
        return carry

    lax.fori_loop(0, tokens // TILE_Q, one_q, 0)
    dk_ref[...] = dka_ref[...].astype(bf16)
    dv_ref[...] = dva_ref[...].astype(bf16)


smem_spec = pl.BlockSpec(memory_space=pltpu.SMEM)
vmem_spec = pl.BlockSpec(memory_space=pltpu.VMEM)


def attend(lows, highs, q, k, v, seg_row, seg_col):
    tokens, width = q.shape
    return pl.pallas_call(
        attend_kernel,
        in_specs=[smem_spec] * 2 + [vmem_spec] * 5,
        out_specs=[vmem_spec] * 3,
        out_shape=[
            jax.ShapeDtypeStruct((tokens, width), bf16),
            jax.ShapeDtypeStruct((width, tokens), f32),
            jax.ShapeDtypeStruct((8, tokens), f32),
        ],
        scratch_shapes=[pltpu.VMEM((width, tokens), bf16), pltpu.VMEM((width, TILE_Q), f32)],
        name="attend",
    )(lows, highs, q, k, v, seg_row, seg_col)


def attend_back(lows, highs, q, k, v, do, attt, lse, seg_row, seg_col):
    tokens, width = q.shape
    return pl.pallas_call(
        attend_back_kernel,
        in_specs=[smem_spec] * 2 + [vmem_spec] * 8,
        out_specs=[vmem_spec] * 3,
        out_shape=[jax.ShapeDtypeStruct((tokens, width), bf16)] * 3,
        scratch_shapes=[
            pltpu.VMEM((width, tokens), bf16),
            pltpu.VMEM((width, TILE_Q), f32),
            pltpu.VMEM((tokens, width), f32),
            pltpu.VMEM((tokens, width), f32),
        ],
        name="attend_back",
    )(lows, highs, q, k, v, do, attt, lse, seg_row, seg_col)


def exact_gelu(values):
    return jax.nn.gelu(values, approximate=False)


def norm_forward(resid, gain, shift):
    row_mean = jnp.mean(resid, axis=1, keepdims=True)
    spread = jnp.mean(resid * resid, axis=1, keepdims=True) - row_mean * row_mean
    inverse = lax.rsqrt(spread + epsilon)
    normed = (resid - row_mean) * inverse
    return (normed * gain + shift, normed, inverse)


def norm_backward(upstream, normed, inverse, gain):
    scaled = upstream * gain
    first_mean = jnp.mean(scaled, axis=1, keepdims=True)
    second_mean = jnp.mean(scaled * normed, axis=1, keepdims=True)
    back_term = inverse * (scaled - first_mean - normed * second_mean)
    return (back_term, jnp.sum(upstream * normed, axis=0), jnp.sum(upstream, axis=0))


def token_sum(tensor):
    return jnp.sum(tensor.astype(f32), axis=0)


def per_device(
    inputs,
    segments,
    query_weight,
    query_bias,
    key_weight,
    value_weight,
    value_bias,
    output_weight,
    output_bias,
    first_gain,
    first_shift,
    expand_weight,
    expand_bias,
    contract_weight,
    contract_bias,
    second_gain,
    second_shift,
    cotangent,
):
    seq_count, rows_here, features = inputs.shape
    lines = lax.axis_size("tp")
    blocks = lax.axis_size("ctx")
    width = query_weight.shape[1]
    hidden = expand_weight.shape[1]
    shard = query_weight.shape[0]
    assert seq_count == lines and blocks == lines
    tokens = segments.shape[1]
    here = rows_here * lines
    groups = range(lines)

    front = gather_rows(jnp.concatenate([query_weight, key_weight, value_weight], 1))
    biases = gather_line(jnp.concatenate([query_bias, value_bias, expand_bias]), "tp")
    x = exchange_blocks(inputs, "tp").reshape(here, features)
    back = gather_rows(
        jnp.concatenate([expand_weight, contract_weight.T, output_weight.T], 1)
    )
    expand = [back[t, :, :hidden] for t in groups]
    contract = [back[t, :, hidden : 2 * hidden] for t in groups]
    output = [back[t, :, 2 * hidden :] for t in groups]

    seg = lax.dynamic_index_in_dim(segments, lax.axis_index("tp"), 0, keepdims=False)
    firsts, lasts = seg[::TILE_Q], seg[TILE_Q - 1 :: TILE_Q]
    before = jnp.sum((seg[None, :] < firsts[:, None]).astype(jnp.int32), axis=1)
    until = jnp.sum((seg[None, :] <= lasts[:, None]).astype(jnp.int32), axis=1)
    lows, highs = before // TILE_K, (until + TILE_K - 1) // TILE_K
    seg_row, seg_col = seg[None, :], seg[:, None]

    none = jnp.zeros((width,), f32)
    projected = jnp.stack(
        [
            (
                dot32(x, front[t], ((1,), (0,)))
                + jnp.concatenate([biases[t, :width], none, biases[t, width : 2 * width]])
            ).astype(bf16)
            for t in groups
        ]
    )
    qkv = exchange_blocks(projected, "ctx").reshape(tokens, 3 * width)
    q, k, v = qkv[:, :width], qkv[:, width : 2 * width], qkv[:, 2 * width :]
    att, attt, lse = attend(lows, highs, q, k, v, seg_row, seg_col)
    att = exchange_blocks(att.reshape(blocks, here, width), "ctx")
    branch = output_bias + sum(dot32(att[t], output[t], ((1,), (1,))) for t in groups)
    middle, middle_normed, middle_inverse = norm_forward(
        x.astype(f32) + branch, first_gain, first_shift
    )
    middle_low = middle.astype(bf16)
    actives, pulls = [], []
    for t in groups:
        preact = dot32(middle_low, expand[t], ((1,), (0,))) + biases[t, 2 * width :]
        active, pull = jax.vjp(exact_gelu, preact)
        actives.append(active.astype(bf16))
        pulls.append(pull)
    feedforward = contract_bias + sum(
        dot32(actives[t], contract[t], ((1,), (1,))) for t in groups
    )
    outputs, final_normed, final_inverse = norm_forward(
        middle + feedforward, second_gain, second_shift
    )
    outputs = exchange_blocks(
        outputs.astype(bf16).reshape(lines, rows_here, features), "tp"
    )

    upstream = exchange_blocks(cotangent, "tp").reshape(here, features).astype(f32)
    final_grad, second_gain_grad, second_shift_grad = norm_backward(
        upstream, final_normed, final_inverse, second_gain
    )
    feed_grad = final_grad.astype(bf16)
    contract_bias_grad = token_sum(feed_grad)
    expand_bias_grads, expand_parts, contract_parts, output_parts = [], [], [], []
    middle_grad = final_grad
    for t in groups:
        active_grad = dot32(feed_grad, contract[t], ((1,), (0,)))
        preact_grad = pulls[t](active_grad)[0].astype(bf16)
        expand_bias_grads.append(token_sum(preact_grad))
        contract_parts.append(dot32(feed_grad, actives[t], ((0,), (0,))).astype(bf16))
        expand_parts.append(dot32(middle_low, preact_grad, ((0,), (0,))).astype(bf16))
        middle_grad = middle_grad + dot32(preact_grad, expand[t], ((1,), (1,)))
    resid_grad, first_gain_grad, first_shift_grad = norm_backward(
        middle_grad, middle_normed, middle_inverse, first_gain
    )
    branch_grad = resid_grad.astype(bf16)
    output_bias_grad = token_sum(branch_grad)
    for t in groups:
        output_parts.append(dot32(branch_grad, att[t], ((0,), (0,))).astype(bf16))
    att_grad = jnp.stack(
        [dot32(branch_grad, output[t], ((1,), (0,))).astype(bf16) for t in groups]
    )
    do = exchange_blocks(att_grad, "ctx").reshape(tokens, width)
    dq, dk, dv = attend_back(lows, highs, q, k, v, do, attt, lse, seg_row, seg_col)
    projected_grad = exchange_blocks(
        jnp.concatenate([dq, dk, dv], 1).reshape(blocks, here, 3 * width), "ctx"
    )
    back_grad = scatter_rows(
        jnp.stack(
            [
                jnp.concatenate([expand_parts[t], contract_parts[t], output_parts[t]], 1)
                for t in groups
            ]
        ),
        shard,
    )
    front_grad = scatter_rows(
        jnp.stack([dot32(x, projected_grad[t], ((0,), (0,))).astype(bf16) for t in groups]),
        shard,
    )
    input_grad = resid_grad + sum(
        dot32(projected_grad[t], front[t], ((1,), (1,))) for t in groups
    )
    input_grad = exchange_blocks(
        input_grad.astype(bf16).reshape(lines, rows_here, features), "tp"
    )

    early = sum_everywhere(
        jnp.concatenate(
            [
                output_bias_grad,
                first_gain_grad,
                first_shift_grad,
                contract_bias_grad,
                second_gain_grad,
                second_shift_grad,
                *expand_bias_grads,
            ]
        )
    )
    late = sum_everywhere(jnp.sum(projected_grad.astype(f32), axis=1))
    line = lax.axis_index("tp")
    own = lax.dynamic_index_in_dim(late, line, 0, keepdims=False)
    whole = early[: 6 * features].reshape(6, features)
    expand_bias_grad = lax.dynamic_slice_in_dim(early, 6 * features + line * hidden, hidden, 0)
    return (
        outputs,
        input_grad,
        front_grad[:, :width],
        own[:width],
        front_grad[:, width : 2 * width],
        front_grad[:, 2 * width :],
        own[2 * width :],
        back_grad[:, 2 * hidden :].T,
        whole[0],
        whole[1],
        whole[2],
        back_grad[:, :hidden],
        expand_bias_grad,
        back_grad[:, hidden : 2 * hidden].T,
        whole[3],
        whole[4],
        whole[5],
    )


def solution(mesh):
    rows = P("fsdp", ("ctx", "tp"), None)
    front, back = P(("fsdp", "ctx"), "tp"), P("tp", ("fsdp", "ctx"))
    return jax.shard_map(
        per_device,
        mesh=mesh,
        in_specs=(
            rows, P("fsdp", None), front, P("tp"), front, front, P("tp"), back, P(), P(), P(),
            front, P("tp"), back, P(), P(), P(), rows,
        ),
        out_specs=(
            rows, rows, front, P("tp"), front, front, P("tp"), back, P(), P(), P(),
            front, P("tp"), back, P(), P(), P(),
        ),
        check_vma=False,
    )
```
